256 devices in a mesh: row: 8 (over x, core), col: 32 (over y, z).
Axes of the slice: x: 4, y: 4, z: 8, core: 2. Of those that a mesh axis runs over, the one named last changes fastest.
Arguments:
- affinity_tiles: bfloat16 [1024, 64, 128, 128], P(('row', 'col'))
- block_columns: int32 [1024, 64], P(('row', 'col')), may hold values from 0 to 127, as said below
- live_counts: int32 [8, 128], P('row', 'col'), may hold values from 1 to 64, 4096 in all within a row
- earlier_blocks: float32 [4, 64, 131072], P(None, None, ('row', 'col')), may hold values from -6 to 6
Outputs:
- new_blocks: float32 [2, 64, 131072], P(None, None, ('row', 'col'))
- triangular_factors: float32 [2, 64, 64], replicated
The draws below stay inside these ranges and needn't reach their ends.
Inputs may be any that keep to these rules, and one draw needn't show every extreme that they name: `block_columns`: slot 0 of every block row names the block row itself; columns name block rows of the same row group. `live_counts`: slots at or past a block row's count are ignored.
All inputs are finite; a program needn't handle non-finite values.
Results may differ from the reference program's by a relative error of at most 0.0059.
Values may be sent and summed in bfloat16 or wider, within the bound.
No kernel may reach another device: no remote copies, remote signals or barrier semaphores. Data moves between devices by JAX's collectives and lax.ppermute only.
A program may use at most 64 MiB of HBM per device.

```python
import math
import jax
import jax.numpy as jnp
import numpy as np
from jax import lax

TILE = 128
B = 64
K = 64
PREV = 4
STEPS = 2
GROUP_BR = 128
NBR = 1024
N_ROWS = 131072
N_ROW = 8


def draw_affinity_tiles(key, part):
    noise_key, diag_key = jax.random.split(key)
    tile_shape = (NBR, K, TILE, TILE)
    noise = jax.random.normal(noise_key, tile_shape, jnp.float32)
    noise = noise * (K * TILE // 2) ** (-0.5)
    row_ids = jnp.arange(NBR, dtype=jnp.float32)
    rising = jnp.exp(math.log(4.0) * row_ids / max(NBR - 1, 1))
    diag_vals = jax.random.uniform(diag_key, (NBR, TILE), jnp.float32, 0.5, 1.5) * rising[:, None]
    on_diag = (jnp.arange(TILE)[:, None] == jnp.arange(TILE)[None, :]).astype(jnp.float32)
    first_slot = (jnp.arange(K) == 0).astype(jnp.float32)
    diag_part = diag_vals[:, None, :, None] * on_diag[None, None, :, :] * first_slot[None, :, None, None]
    return (noise + diag_part).astype(jnp.bfloat16)


def draw_block_columns(key, part):
    own_block = jnp.arange(NBR, dtype=jnp.int32) % GROUP_BR
    offsets = jax.random.randint(key, (NBR, K), 1, GROUP_BR, dtype=jnp.int32)
    spread = (own_block[:, None] + offsets) % GROUP_BR
    slot_ids = jnp.arange(K, dtype=jnp.int32)[None, :]
    return jnp.where(slot_ids == 0, own_block[:, None], spread)


def shard_levels(stream_key, dims, shards, low, top_value):
    loudness = 1.0
    for dim, parts in shards:
        draws = jax.random.uniform(jax.random.fold_in(jax.random.fold_in(stream_key, 6), dim), (parts,), jnp.float32, low / len(shards), top_value / len(shards))
        loudness = loudness * jnp.repeat(jnp.exp(draws), dims[dim] // parts).reshape((-1,) + (1,) * (len(dims) - 1 - dim))
    return loudness


def length_profile(count, total, bound, lean):
    weights = [(1 << 20) // math.isqrt(standing ** lean) + 1 for standing in range(2, count + 1)]
    rest, counts = total - bound - (count - 1), [1] * (count - 1)
    while rest > 0:
        free = [i for i in range(count - 1) if counts[i] < bound]
        whole, budget = sum([weights[i] for i in free]), rest
        for i in free:
            addition = min(bound - counts[i], max(1, budget * weights[i] // whole), rest)
            counts[i] = counts[i] + addition
            rest = rest - addition
    return np.array([bound] + counts)


def ragged(stream_key, amount, total, limit, slope):
    if amount == 2:
        one = jax.random.randint(stream_key, (), max(1, total - limit), min(limit, total - 1) + 1)
        return jnp.stack([one, total - one])
    sizes = jnp.asarray(length_profile(amount, total, limit, slope), jnp.int32)
    twos = (amount - 1) // 2
    giver, receiver = sizes[1:1 + 2 * twos:2], sizes[2:2 + 2 * twos:2]
    slack = jnp.minimum(giver - 1, limit - receiver)
    moved = jax.random.randint(jax.random.fold_in(stream_key, 1), (twos,), 0, 1 << 20) % (slack + 1)
    sizes = sizes.at[1:1 + 2 * twos:2].set(giver - moved).at[2:2 + 2 * twos:2].set(receiver + moved)
    return sizes[jax.random.permutation(jax.random.fold_in(stream_key, 2), amount)]


def gaussian(rng, dims, scale, most, cuts=(), kind=jnp.bfloat16):
    result = scale * jax.random.normal(rng, dims, jnp.float32)
    if cuts:
        result = result * shard_levels(rng, dims, cuts, -0.22, 0.18)
    return jnp.clip(result, -most, most).astype(kind)


def setup_inputs(seed: int = 0) -> dict:
    keys = jax.random.split(jax.random.key(seed), 5)
    return {
        "affinity_tiles": draw_affinity_tiles(jax.random.fold_in(keys[4], 71), 0),
        "block_columns": draw_block_columns(jax.random.fold_in(keys[4], 71), 0),
        "live_counts": jax.vmap(lambda own: ragged(own, GROUP_BR, GROUP_BR * K // 2, K, 2))(jax.random.split(keys[2], N_ROW)).reshape((N_ROW, GROUP_BR)).astype(jnp.int32),
        "earlier_blocks": gaussian(keys[3], (PREV, B, N_ROWS), 1.0, 6.0, ((2, 256),), jnp.float32),
    }


def apply_operator(current_half, affinity_tiles, block_columns, live_counts):
    column_blocks = current_half.reshape(B, NBR, TILE)
    row_ids = jnp.arange(NBR, dtype=jnp.int32)
    global_cols = (row_ids // GROUP_BR * GROUP_BR)[:, None] + block_columns
    live_mask = jnp.arange(K, dtype=jnp.int32)[None, :] < live_counts.reshape(NBR)[:, None]
    block_size = 16 if NBR % 16 == 0 else 1
    block_count = NBR // block_size

    def one_block(pieces):
        tile_part, col_part, mask_part = pieces
        picked = jnp.take(column_blocks, col_part, axis=1).astype(jnp.float32)
        picked = jnp.where(mask_part[None, :, :, None], picked, jnp.zeros((), jnp.float32))
        return jnp.einsum('rsij,brsj->bri', tile_part.astype(jnp.float32), picked)
    results = lax.map(one_block, (affinity_tiles.reshape(block_count, block_size, K, TILE, TILE), global_cols.reshape(block_count, block_size, K), live_mask.reshape(block_count, block_size, K)))
    return jnp.transpose(results, (1, 0, 2, 3)).reshape(B, N_ROWS)

def reference(affinity_tiles, block_columns, live_counts, earlier_blocks):
    known_list = [earlier_blocks[i] for i in range(PREV)]
    current = earlier_blocks[PREV - 1]
    fresh_list = []
    factor_list = []
    for step_index in range(STEPS):
        current_half = current.astype(jnp.bfloat16)
        product = apply_operator(current_half, affinity_tiles, block_columns, live_counts)
        known = jnp.stack(known_list)
        projections = jnp.einsum('mbn,cn->mbc', known, product, precision=lax.Precision.HIGHEST) / N_ROWS
        residual = product - jnp.einsum('mbn,mbc->cn', known, projections, precision=lax.Precision.HIGHEST)
        gram = jnp.dot(residual, residual.T, precision=lax.Precision.HIGHEST) / N_ROWS
        factor_low = jnp.linalg.cholesky(gram)
        fresh = jax.scipy.linalg.solve_triangular(factor_low, residual, lower=True)
        fresh_list.append(fresh)
        factor_list.append(factor_low.T)
        known_list.append(fresh)
        current = fresh
    return (jnp.stack(fresh_list), jnp.stack(factor_list))
```

```python
import functools

import jax
import jax.numpy as jnp
from jax import lax
from jax.experimental import pallas as pl
from jax.experimental.pallas import tpu as pltpu
from jax.sharding import PartitionSpec as P

STEPS = 2
NX, NY, NZ, NC = 4, 4, 8, 2
CHUNK = 8
HI = lax.Precision.HIGHEST


def col_id(y, z):
    return (y % NY) * NZ + z % NZ


def row_id(x, core):
    return (x % NX) * NC + core % NC


Y_UP = [(col_id(y, z), col_id(y + 1, z)) for y in range(NY) for z in range(NZ)]
Y_DOWN = [(col_id(y, z), col_id(y - 1, z)) for y in range(NY) for z in range(NZ)]
CORE_SWAP = [(row_id(x, c), row_id(x, c + 1)) for x in range(NX) for c in range(NC)]
Z_GROUPS = [[col_id(y, z) for z in range(NZ)] for y in range(NY)]
X_GROUPS = [[row_id(x, c) for x in range(NX)] for c in range(NC)]


def to_all(a, axis, count, groups=None):
    copies = jnp.broadcast_to(a[None], (count,) + a.shape)
    return lax.all_to_all(copies, axis, 0, 0, axis_index_groups=groups, tiled=True)


def gather_group(half):
    own = to_all(half, "col", NZ, Z_GROUPS)
    below = lax.ppermute(own, "col", Y_UP)
    above = lax.ppermute(own, "col", Y_DOWN)
    far_low = lax.ppermute(below[: NZ // 2], "col", Y_UP)
    far_high = lax.ppermute(above[NZ // 2 :], "col", Y_DOWN)
    everything = jnp.concatenate([own, above, far_low, far_high, below], 0)
    return everything.reshape((-1,) + half.shape[1:])


def sum_everywhere(a):
    rows = a.shape[0] // 2
    core = lax.axis_index("row") % NC
    kept = lax.dynamic_slice_in_dim(a, core * rows, rows, 0)
    sent = lax.dynamic_slice_in_dim(a, (1 - core) * rows, rows, 0)
    part = kept + lax.ppermute(sent, "row", CORE_SWAP)
    part = part.reshape(NY * NZ, rows // (NY * NZ), a.shape[1])
    piece = jnp.sum(lax.all_to_all(part, "col", 0, 0, tiled=True), 0)
    piece = jnp.sum(to_all(piece, "row", NX, X_GROUPS), 0)
    mine = to_all(piece, "col", NY * NZ).reshape(rows, a.shape[1])
    other = lax.ppermute(mine, "row", CORE_SWAP)
    first = jnp.where(core == 0, mine, other)
    second = jnp.where(core == 0, other, mine)
    return jnp.concatenate([first, second], 0)


def apply_kernel(block_rows, slots, picks, counts, group, tiles, out, store, sems):
    chunks = slots // CHUNK

    def copy(r, k):
        at = pl.ds(k * CHUNK, CHUNK)
        return pltpu.make_async_copy(tiles.at[r, at], store.at[r, at], sems.at[r, k])

    for r in range(block_rows):
        for k in range(chunks):

            @pl.when(k * CHUNK < counts[r])
            def _():
                copy(r, k).start()

    for r in range(block_rows):
        live = counts[r]

        def step(k, total):
            copy(r, k).wait()
            sides = []
            for j in range(CHUNK):
                slot = k * CHUNK + j
                side = group[picks[r * slots + slot]]
                sides.append(jnp.where(slot < live, side, jnp.zeros_like(side)))
            left = jnp.concatenate(sides, 1)
            right = jnp.concatenate([store[r, k * CHUNK + j] for j in range(CHUNK)], 1)
            return total + lax.dot_general(
                left, right, (((1,), (1,)), ((), ())), preferred_element_type=jnp.float32
            )

        width, size = group.shape[1], group.shape[2]
        total = lax.fori_loop(
            0, (live + CHUNK - 1) // CHUNK, step, jnp.zeros((width, size), jnp.float32)
        )
        out[:, r * size : (r + 1) * size] = total


def apply_tiles(tiles, picks, counts, group):
    block_rows, slots, size, _ = tiles.shape
    width = group.shape[1]
    return pl.pallas_call(
        functools.partial(apply_kernel, block_rows, slots),
        out_shape=jax.ShapeDtypeStruct((width, block_rows * size), jnp.float32),
        in_specs=[
            pl.BlockSpec(memory_space=pltpu.SMEM),
            pl.BlockSpec(memory_space=pltpu.SMEM),
            pl.BlockSpec(memory_space=pltpu.VMEM),
            pl.BlockSpec(memory_space=pl.ANY),
        ],
        out_specs=pl.BlockSpec(memory_space=pltpu.VMEM),
        scratch_shapes=[
            pltpu.VMEM((block_rows, slots, size, size), tiles.dtype),
            pltpu.SemaphoreType.DMA((block_rows, slots // CHUNK)),
        ],
        compiler_params=pltpu.CompilerParams(vmem_limit_bytes=32 << 20),
        name="apply_tiles",
    )(picks, counts, group, tiles)


def split_blocks(a, size):
    return jnp.transpose(a.reshape(a.shape[0], -1, size), (1, 0, 2))


def mm(a, b):
    return jnp.dot(a, b, precision=HI)


def pair_up(blocks):
    if len(blocks) % 2:
        blocks = blocks + [jnp.zeros_like(blocks[0])]
    rows = [jnp.concatenate(blocks[i : i + 2], 1) for i in range(0, len(blocks), 2)]
    return jnp.concatenate(rows, 0)


def unpair(a, count, b):
    return [a[i // 2 * b : (i // 2 + 1) * b, i % 2 * b : (i % 2 + 1) * b] for i in range(count)]


def on_device(tiles, block_columns, live_counts, earlier):
    block_rows, slots, size, _ = tiles.shape
    prev, b, rows_here = earlier.shape
    total_rows = rows_here * lax.axis_size("row") * lax.axis_size("col")
    counts = live_counts.reshape(block_rows)
    here_y = lax.axis_index("col") // NZ
    owner = block_columns // block_rows
    turn = (owner // NZ - here_y) % NY
    picks = (turn * NZ + owner % NZ) * block_rows + block_columns % block_rows
    picks = picks.reshape(-1)

    known = earlier.reshape(prev * b, rows_here)
    group = gather_group(split_blocks(earlier[-1].astype(jnp.bfloat16), size))
    product = apply_tiles(tiles, picks, counts, group)

    def block(a, i):
        return a[i * b : (i + 1) * b]

    stack = jnp.concatenate([known, product], 0)
    inner = mm(stack, stack.T) / total_rows
    pairs = [(i, j) for i in range(prev + 1) for j in range(i, prev + 1)]
    blocks = [inner[i * b : (i + 1) * b, j * b : (j + 1) * b] for i, j in pairs]
    sums = unpair(sum_everywhere(pair_up(blocks)), len(blocks), b)
    table = dict(zip(pairs, sums))
    proj = jnp.concatenate([table[i, prev] for i in range(prev)], 0)
    own = jnp.concatenate(
        [
            jnp.concatenate(
                [table[i, j] if i <= j else table[j, i].T for j in range(prev)], 1
            )
            for i in range(prev)
        ],
        0,
    )
    spread = mm(own, proj)
    gram = table[prev, prev] + mm(proj.T, spread - 2 * proj)
    residual = product - mm(proj.T, known)
    factor = jnp.linalg.cholesky(gram)
    eye = jnp.eye(b, dtype=jnp.float32)
    inverse = jax.scipy.linalg.solve_triangular(factor, eye, lower=True)
    fresh = mm(inverse, residual)
    factors = [factor.T]
    fresh_list = [fresh]

    group = gather_group(split_blocks(fresh.astype(jnp.bfloat16), size))
    product = apply_tiles(tiles, picks, counts, group)
    known = jnp.concatenate([known, fresh], 0)
    stack = jnp.concatenate([known, product], 0)
    inner = mm(stack, product.T) / total_rows
    blocks = [block(inner, i) for i in range(prev + 2)]
    blocks += [jnp.zeros_like(blocks[0])] * (16 - len(blocks))
    sums = unpair(sum_everywhere(pair_up(blocks)), prev + 2, b)
    proj2 = jnp.concatenate(sums[: prev + 1], 0)
    cross = mm(proj - spread, inverse.T)
    top = jnp.concatenate([own, cross], 1)
    low = jnp.concatenate([cross.T, eye], 1)
    spread2 = mm(jnp.concatenate([top, low], 0), proj2)
    gram = sums[prev + 1] + mm(proj2.T, spread2 - 2 * proj2)
    residual = product - mm(proj2.T, known)
    factor = jnp.linalg.cholesky(gram)
    fresh_list.append(jax.scipy.linalg.solve_triangular(factor, residual, lower=True))
    factors.append(factor.T)
    return (jnp.stack(fresh_list), jnp.stack(factors))


def solution(mesh):
    return jax.shard_map(
        on_device,
        mesh=mesh,
        in_specs=(
            P(("row", "col"), None, None, None),
            P(("row", "col"), None),
            P("row", "col"),
            P(None, None, ("row", "col")),
        ),
        out_specs=(P(None, None, ("row", "col")), P()),
        check_vma=False,
    )
```

```python
import functools

import jax
import jax.numpy as jnp
from jax import lax
from jax.experimental import pallas as pl
from jax.experimental.pallas import tpu as pltpu
from jax.sharding import PartitionSpec as P

STEPS = 2
NX, NY, NZ, NC = 4, 4, 8, 2
SUB = 8
GROUP = 4
AT_ONCE = 4
FAR = 2
VECTORS = 32
CODE = 128
DEAD = CODE - 1
HI = lax.Precision.HIGHEST


def col_id(y, z):
    return (y % NY) * NZ + z % NZ


def row_id(x, core):
    return (x % NX) * NC + core % NC


Y_UP = [(col_id(y, z), col_id(y + 1, z)) for y in range(NY) for z in range(NZ)]
Y_DOWN = [(col_id(y, z), col_id(y - 1, z)) for y in range(NY) for z in range(NZ)]
Z_GROUPS = [[col_id(y, z) for z in range(NZ)] for y in range(NY)]
XY_GROUPS = [
    [row_id(x, c) * NY * NZ + col_id(y, z) for x in range(NX) for y in range(NY)]
    for c in range(NC)
    for z in range(NZ)
]
CZ_GROUPS = [
    [row_id(x, c) * NY * NZ + col_id(y, z) for c in range(NC) for z in range(NZ)]
    for x in range(NX)
    for y in range(NY)
]
ALL = ("row", "col")


def to_all(a, axis, count, groups=None):
    copies = jnp.broadcast_to(a[None], (count,) + a.shape)
    return lax.all_to_all(copies, axis, 0, 0, axis_index_groups=groups, tiled=True)


def gather_group(half):
    own = to_all(half, "col", NZ, Z_GROUPS)
    below = lax.ppermute(own, "col", Y_UP)
    above = lax.ppermute(own, "col", Y_DOWN)
    far_low = lax.ppermute(below[: NZ // 2], "col", Y_UP)
    far_high = lax.ppermute(above[NZ // 2 :], "col", Y_DOWN)
    return own, above, far_low, far_high, below


def sum_everywhere(a):
    members = NX * NY
    part = a.reshape(members, a.shape[0] // members, a.shape[1])
    piece = lax.all_to_all(part, ALL, 0, 0, axis_index_groups=XY_GROUPS, tiled=True)
    piece = jnp.sum(piece, 0)
    piece = jnp.sum(to_all(piece, ALL, NC * NZ, CZ_GROUPS), 0)
    return to_all(piece, ALL, members, XY_GROUPS).reshape(a.shape)


def dot_nt(a, b):
    return lax.dot_general(
        a, b, (((1,), (1,)), ((), ())), precision=HI, preferred_element_type=jnp.float32
    )


def dot_nn(a, b):
    return lax.dot_general(
        a, b, (((1,), (0,)), ((), ())), precision=HI, preferred_element_type=jnp.float32
    )


def prepare_kernel(slots, picks, counts, near, near_rows, far, far_rows, totals):
    block_rows = counts.shape[0]

    def sort(r, carry):
        def one(s, carry):
            a, f = carry
            pick = picks[r * slots + s]
            turn = pick // VECTORS
            beyond = (turn == FAR).astype(jnp.int32)
            after = (turn > FAR).astype(jnp.int32)
            near[a] = s * CODE + pick - after * VECTORS
            far[f] = s * CODE + pick - FAR * VECTORS
            return a + 1 - beyond, f + beyond

        def fill(table, rows, start, end):
            for j in range(GROUP):
                table[end + j] = DEAD
            stop = (end + GROUP - 1) // GROUP

            def mark(c, _):
                rows[c] = r
                return 0

            lax.fori_loop(start // GROUP, stop, mark, 0)
            return stop * GROUP

        a, f = lax.fori_loop(0, counts[r], one, carry)
        return fill(near, near_rows, carry[0], a), fill(far, far_rows, carry[1], f)

    a, f = lax.fori_loop(0, block_rows, sort, (jnp.int32(0), jnp.int32(0)))
    for n, (table, rows, end) in enumerate(((near, near_rows, a), (far, far_rows, f))):
        for j in range(GROUP * AT_ONCE):
            table[end + j] = DEAD
        for j in range(AT_ONCE):
            rows[end // GROUP + j] = 0
        totals[n] = (end + GROUP * AT_ONCE - 1) // (GROUP * AT_ONCE)


def prepare(tiles, picks, counts):
    block_rows, slots = tiles.shape[:2]
    smem = pl.BlockSpec(memory_space=pltpu.SMEM)
    entries = block_rows * (slots + GROUP) + 2 * GROUP * AT_ONCE
    table = jax.ShapeDtypeStruct((entries,), jnp.int32)
    rows = jax.ShapeDtypeStruct((entries // GROUP,), jnp.int32)
    return pl.pallas_call(
        functools.partial(prepare_kernel, slots),
        out_shape=(
            table,
            rows,
            table,
            rows,
            jax.ShapeDtypeStruct((2,), jnp.int32),
        ),
        in_specs=[smem, smem],
        out_specs=(smem,) * 5,
        compiler_params=pltpu.CompilerParams(vmem_limit_bytes=16 << 20),
        cost_estimate=pl.CostEstimate(flops=0, bytes_accessed=8 << 20, transcendentals=0),
        name="prepare",
    )(picks, counts)


def multiply(table, rows, trips, parts, store, group, sems, total):
    copies, start = [], 0
    for n, part in enumerate(parts):
        at = pl.ds(start, part.shape[0])
        copies.append(pltpu.make_async_copy(part, group.at[at], sems.at[n]))
        start += part.shape[0]
    for c in copies:
        c.start()
    group[start] = jnp.zeros(group.shape[1:], group.dtype)
    for c in copies:
        c.wait()
    block_rows = group.shape[1]
    dead = start * block_rows

    def step(t, carry):
        for c in range(AT_ONCE):
            chunk = t * AT_ONCE + c
            r = rows[chunk]
            left, right = [], []
            for j in range(GROUP):
                code = table[chunk * GROUP + j]
                pick = jnp.minimum(code % CODE, dead)
                left.append(group[pick // block_rows, pick % block_rows])
                right.append(store[r, code // CODE])
            total[r] += lax.dot_general(
                jnp.concatenate(left, 1),
                jnp.concatenate(right, 1),
                (((1,), (1,)), ((), ())),
                preferred_element_type=jnp.float32,
            )
        return carry

    lax.fori_loop(0, trips, step, 0)


def near_kernel(table, rows, totals, own, above, below, store, total, group, sems):
    total[...] = jnp.zeros_like(total)
    multiply(table, rows, totals[0], (own, above, below), store, group, sems, total)


def far_kernel(scale, table, rows, totals, low, high, store, start, known, *refs):
    out, inner, group, sems, total = refs
    total[...] = start[...]
    multiply(table, rows, totals[1], (low, high), store, group, sems, total)
    product = jnp.concatenate([total[r] for r in range(total.shape[0])], 1)
    out[...] = product
    width = product.shape[0]
    both = jnp.concatenate([dot_nt(product, known[...]), dot_nt(product, product)], 1) * scale
    lanes = inner.shape[1]
    for n in range(0, both.shape[1], lanes):
        piece = both[:, n : n + lanes]
        row = n // lanes * width
        inner[row : row + width, : piece.shape[1]] = piece
        if piece.shape[1] < lanes:
            inner[row : row + width, piece.shape[1] :] = jnp.zeros(
                (width, lanes - piece.shape[1]), jnp.float32
            )


def apply_tiles(store, prepared, parts, known, scale):
    near, near_rows, far, far_rows, totals = prepared
    own, above, low, high, below = parts
    block_rows, _, size, _ = store.shape
    width = own.shape[2]
    vmem, smem = pl.BlockSpec(memory_space=pltpu.VMEM), pl.BlockSpec(memory_space=pltpu.SMEM)
    anywhere = pl.BlockSpec(memory_space=pl.ANY)
    total = jax.ShapeDtypeStruct((block_rows, width, size), jnp.float32)

    def scratch(*parts):
        held = sum(p.shape[0] for p in parts) + 1
        return [
            pltpu.VMEM((held,) + own.shape[1:], own.dtype),
            pltpu.SemaphoreType.DMA((len(parts),)),
        ]

    params = pltpu.CompilerParams(vmem_limit_bytes=20 << 20)
    start = pl.pallas_call(
        near_kernel,
        out_shape=total,
        in_specs=[smem] * 3 + [anywhere] * 3 + [vmem],
        out_specs=vmem,
        scratch_shapes=scratch(own, above, below),
        compiler_params=params,
        cost_estimate=pl.CostEstimate(
            flops=1 << 29, bytes_accessed=10 << 20, transcendentals=0
        ),
        name="near_tiles",
    )(near, near_rows, totals, own, above, below, store)
    pieces = -(-(known.shape[0] + width) // size)
    return pl.pallas_call(
        functools.partial(far_kernel, scale),
        out_shape=(
            jax.ShapeDtypeStruct((width, block_rows * size), jnp.float32),
            jax.ShapeDtypeStruct((pieces * width, size), jnp.float32),
        ),
        in_specs=[smem] * 3 + [anywhere] * 2 + [vmem] * 3,
        out_specs=(vmem, vmem),
        scratch_shapes=scratch(low, high) + [pltpu.VMEM(total.shape, total.dtype)],
        compiler_params=params,
        name="far_tiles",
    )(far, far_rows, totals, low, high, store, start, known)


def factor(gram):
    n = gram.shape[0]
    across = 2 * n
    row_ids = lax.broadcasted_iota(jnp.int32, (n, n), 0)
    col_ids = lax.broadcasted_iota(jnp.int32, (n, n), 1)
    eye = jnp.where(row_ids == col_ids, 1.0, 0.0).astype(jnp.float32)
    wide = jnp.concatenate([gram, eye], 1)
    parts = [wide[i : i + SUB] for i in range(0, n, SUB)]
    sub = lax.broadcasted_iota(jnp.int32, (SUB, across), 0)

    def lane(a, k):
        return jnp.broadcast_to(a[:, k : k + 1], (SUB, across))

    for k in range(0, n, 2):
        home, at = divmod(k, SUB)
        one = jnp.broadcast_to(parts[home][at : at + 1], (SUB, across))
        two = jnp.broadcast_to(parts[home][at + 1 : at + 2], (SUB, across))
        head, beside = lane(one, k), lane(one, k + 1)
        head_inv = 1.0 / head
        link = lane(two, k) * head_inv
        tail_inv = 1.0 / (lane(two, k + 1) - link * beside)
        two = two - link * one
        for i in range(home, len(parts)):
            first = lane(parts[i], k) * head_inv
            second = (lane(parts[i], k + 1) - first * beside) * tail_inv
            if i == home:
                first = jnp.where(sub > at, first, 0.0)
                second = jnp.where(sub > at + 1, second, 0.0)
            parts[i] = parts[i] - first * one - second * two
    wide = jnp.concatenate(parts, 0)
    upper = wide[:, :n]
    diag = jnp.sum(jnp.where(row_ids == col_ids, upper, 0.0), 1, keepdims=True)
    scale = lax.rsqrt(diag)
    upper = jnp.where(row_ids <= col_ids, upper * scale, 0.0)
    lower = jnp.where(row_ids >= col_ids, wide[:, n:] * scale, 0.0)
    return upper, lower


def block_of(ref, i, b):
    return ref[i // 2 * b : (i // 2 + 1) * b, i % 2 * b : (i % 2 + 1) * b]


def known_inner(sums, prev, b):
    table, n = {}, 0
    for i in range(prev):
        for j in range(i, prev):
            table[i, j] = block_of(sums, n, b)
            n += 1
    rows = []
    for i in range(prev):
        row = [table[i, j] if i <= j else table[j, i].T for j in range(prev)]
        rows.append(jnp.concatenate(row, 1))
    return jnp.concatenate(rows, 0)


def first_kernel(sums, product, known, fresh, half, upper, cross):
    b = product.shape[0]
    prev = known.shape[0] // b
    count = prev * (prev + 1) // 2
    own = known_inner(sums, prev, b)
    proj = jnp.concatenate([block_of(sums, count + i, b) for i in range(prev)], 1)
    spread = dot_nn(proj, own)
    gram = block_of(sums, count + prev, b) + dot_nt(spread - 2.0 * proj, proj)
    residual = product[...] - dot_nn(proj, known[...])
    up, inverse = factor(gram)
    new = dot_nn(inverse, residual)
    fresh[...] = new
    upper[...] = up
    cross[...] = dot_nn(inverse, proj - spread)
    size = half.shape[2]
    for i in range(half.shape[0]):
        half[i] = new[:, i * size : (i + 1) * size].astype(half.dtype)


def last_kernel(sums, later, cross, product, known, fresh, first_upper, out, uppers):
    b = product.shape[0]
    prev = known.shape[0] // b
    own = known_inner(sums, prev, b)
    old = jnp.concatenate([block_of(later, i, b) for i in range(prev)], 1)
    new = block_of(later, prev, b)
    spread = dot_nn(old, own) + dot_nn(new, cross[...])
    spread_new = dot_nt(old, cross[...]) + new
    gram = (
        block_of(later, prev + 1, b)
        + dot_nt(spread - 2.0 * old, old)
        + dot_nt(spread_new - 2.0 * new, new)
    )
    residual = product[...] - dot_nn(old, known[...]) - dot_nn(new, fresh[...])
    up, inverse = factor(gram)
    out[0] = fresh[...]
    out[1] = dot_nn(inverse, residual)
    uppers[0] = first_upper[...]
    uppers[1] = up


def on_device(tiles, block_columns, live_counts, earlier):
    block_rows, slots, size, _ = tiles.shape
    prev, b, rows_here = earlier.shape
    scale = 1.0 / (rows_here * lax.axis_size("row") * lax.axis_size("col"))
    counts = live_counts.reshape(block_rows)
    here_y = lax.axis_index("col") // NZ
    owner = block_columns // block_rows
    turn = (owner // NZ - here_y) % NY
    picks = (turn * NZ + owner % NZ) * block_rows + block_columns % block_rows
    picks = picks.reshape(-1)
    vmem = pl.BlockSpec(memory_space=pltpu.VMEM)
    f32 = jnp.float32
    known = earlier.reshape(prev * b, rows_here)
    prepared = prepare(tiles, picks, counts)

    def split(a):
        return jnp.transpose(a.reshape(b, block_rows, size), (1, 0, 2))

    parts = gather_group(split(earlier[-1].astype(jnp.bfloat16)))
    inner = jnp.dot(known, known.T, precision=HI) * scale
    blocks = [
        inner[i * b : (i + 1) * b, j * b : (j + 1) * b]
        for i in range(prev)
        for j in range(i, prev)
    ]
    old = [jnp.concatenate(blocks[i : i + 2], 1) for i in range(0, len(blocks), 2)]
    product, mixed = apply_tiles(tiles, prepared, parts, known, scale)
    sums = sum_everywhere(jnp.concatenate(old + [mixed], 0))
    fresh, half, upper, cross = pl.pallas_call(
        first_kernel,
        out_shape=(
            jax.ShapeDtypeStruct((b, rows_here), f32),
            jax.ShapeDtypeStruct((block_rows, b, size), jnp.bfloat16),
            jax.ShapeDtypeStruct((b, b), f32),
            jax.ShapeDtypeStruct((b, prev * b), f32),
        ),
        in_specs=[vmem] * 3,
        out_specs=(vmem,) * 4,
        compiler_params=pltpu.CompilerParams(vmem_limit_bytes=20 << 20),
        name="first_step",
    )(sums, product, known)

    parts = gather_group(half)
    basis = jnp.concatenate([known, fresh], 0)
    product, mixed = apply_tiles(tiles, prepared, parts, basis, scale)
    mixed = jnp.concatenate([mixed, jnp.zeros((256 - mixed.shape[0], size), f32)], 0)
    later = sum_everywhere(mixed)
    return pl.pallas_call(
        last_kernel,
        out_shape=(
            jax.ShapeDtypeStruct((STEPS, b, rows_here), f32),
            jax.ShapeDtypeStruct((STEPS, b, b), f32),
        ),
        in_specs=[vmem] * 7,
        out_specs=(vmem, vmem),
        compiler_params=pltpu.CompilerParams(vmem_limit_bytes=20 << 20),
        name="last_step",
    )(sums, later, cross, product, known, fresh, upper)


def solution(mesh):
    return jax.shard_map(
        on_device,
        mesh=mesh,
        in_specs=(
            P(("row", "col"), None, None, None),
            P(("row", "col"), None),
            P("row", "col"),
            P(None, None, ("row", "col")),
        ),
        out_specs=(P(None, None, ("row", "col")), P()),
        check_vma=False,
    )
```

```python
import functools

import jax
import jax.numpy as jnp
from jax import lax
from jax.experimental import pallas as pl
from jax.experimental.pallas import tpu as pltpu
from jax.sharding import PartitionSpec as P

STEPS = 2
NX, NY, NZ, NC = 4, 4, 8, 2
SUB = 8
PIVOTS = 4
GROUP, GROUP_BITS = 4, 2
AT_ONCE, TRIP_BITS = 8, 5
VECTORS, VECTOR_BITS = 32, 5
DEAD = (VECTORS, 2 * VECTORS, VECTORS)
CODE, CODE_BITS = 128, 7
HI = lax.Precision.HIGHEST


def col_id(y, z):
    return (y % NY) * NZ + z % NZ


def row_id(x, core):
    return (x % NX) * NC + core % NC


Y_UP = [(col_id(y, z), col_id(y + 1, z)) for y in range(NY) for z in range(NZ)]
Y_DOWN = [(col_id(y, z), col_id(y - 1, z)) for y in range(NY) for z in range(NZ)]
Z_GROUPS = [[col_id(y, z) for z in range(NZ)] for y in range(NY)]
XY_GROUPS = [
    [row_id(x, c) * NY * NZ + col_id(y, z) for x in range(NX) for y in range(NY)]
    for c in range(NC)
    for z in range(NZ)
]
CZ_GROUPS = [
    [row_id(x, c) * NY * NZ + col_id(y, z) for c in range(NC) for z in range(NZ)]
    for x in range(NX)
    for y in range(NY)
]
ALL = ("row", "col")


def to_all(a, axis, count, groups=None):
    copies = jnp.broadcast_to(a[None], (count,) + a.shape)
    return lax.all_to_all(copies, axis, 0, 0, axis_index_groups=groups, tiled=True)


def gather_beside(own):
    first, last = own[: NZ // 2], own[NZ // 2 :]
    onward = lax.ppermute(first, "col", Y_UP), lax.ppermute(last, "col", Y_DOWN)
    rest = lax.ppermute(last, "col", Y_UP), lax.ppermute(first, "col", Y_DOWN)
    return onward, rest


def gather_beyond(onward):
    return lax.ppermute(onward[0], "col", Y_UP), lax.ppermute(onward[1], "col", Y_DOWN)


def sum_everywhere(a):
    members = NX * NY
    part = a.reshape(members, a.shape[0] // members, a.shape[1])
    piece = lax.all_to_all(part, ALL, 0, 0, axis_index_groups=XY_GROUPS, tiled=True)
    piece = jnp.sum(piece, 0)
    piece = jnp.sum(to_all(piece, ALL, NC * NZ, CZ_GROUPS), 0)
    return to_all(piece, ALL, members, XY_GROUPS).reshape(a.shape)


def dot_nt(a, b):
    return lax.dot_general(
        a, b, (((1,), (1,)), ((), ())), precision=HI, preferred_element_type=jnp.float32
    )


def dot_nn(a, b):
    return lax.dot_general(
        a, b, (((1,), (0,)), ((), ())), precision=HI, preferred_element_type=jnp.float32
    )


def prepare_kernel(slots, picks, counts, *refs):
    block_rows = counts.shape[0]
    tables, rows, totals = refs[:3], refs[3:6], refs[6]

    def sort(r, ends):
        def one(s, ends):
            pick = picks[r * slots + s]
            turn = pick >> VECTOR_BITS
            tile = (r * slots + s) * CODE + (pick & (VECTORS - 1))
            tables[0][ends[0]] = tile
            tables[1][ends[1]] = tile + ((turn >> 1) << VECTOR_BITS)
            tables[2][ends[2]] = tile
            return (
                ends[0] + jnp.where(turn == 0, 1, 0),
                ends[1] + (turn & 1),
                ends[2] + jnp.where(turn == 2, 1, 0),
            )

        starts, stops = ends, []
        ends = lax.fori_loop(0, counts[r], one, ends)
        for table, row, start, end, dead in zip(tables, rows, starts, ends, DEAD):
            for j in range(GROUP):
                table[end + j] = r * slots * CODE + dead
            stop = (end + GROUP - 1) >> GROUP_BITS

            def mark(c, _, row=row):
                row[c] = r
                return 0

            lax.fori_loop(start >> GROUP_BITS, stop, mark, 0)
            stops.append(stop << GROUP_BITS)
        return tuple(stops)

    ends = lax.fori_loop(0, block_rows, sort, (jnp.int32(0),) * 3)
    for n, (table, row, end, dead) in enumerate(zip(tables, rows, ends, DEAD)):
        for j in range(GROUP * AT_ONCE):
            table[end + j] = dead
        for j in range(AT_ONCE):
            row[(end >> GROUP_BITS) + j] = 0
        totals[n] = (end + GROUP * AT_ONCE - 1) >> TRIP_BITS


def prepare(picks, counts, slots):
    block_rows = counts.shape[0]
    smem = pl.BlockSpec(memory_space=pltpu.SMEM)
    entries = block_rows * (slots + GROUP) + 2 * GROUP * AT_ONCE
    table = jax.ShapeDtypeStruct((entries,), jnp.int32)
    rows = jax.ShapeDtypeStruct((entries // GROUP,), jnp.int32)
    out = pl.pallas_call(
        functools.partial(prepare_kernel, slots),
        out_shape=(table,) * 3 + (rows,) * 3 + (jax.ShapeDtypeStruct((3,), jnp.int32),),
        in_specs=[smem, smem],
        out_specs=(smem,) * 7,
        compiler_params=pltpu.CompilerParams(vmem_limit_bytes=16 << 20),
        cost_estimate=pl.CostEstimate(flops=0, bytes_accessed=8 << 20, transcendentals=0),
        name="prepare",
    )(picks, counts)
    return [(out[n], out[3 + n], out[6]) for n in range(3)]


def multiply(table, rows, trips, parts, store, group, sems, total):
    copies, start = [], 0
    for n, part in enumerate(parts):
        at = pl.ds(start, part.shape[0])
        copies.append(pltpu.make_async_copy(part, group.at[at], sems.at[n]))
        start += part.shape[0]
    for c in copies:
        c.start()
    group[start] = jnp.zeros(group.shape[1:], group.dtype)
    for c in copies:
        c.wait()

    def step(t, carry):
        for c in range(AT_ONCE):
            chunk = t * AT_ONCE + c
            left, right = [], []
            for j in range(GROUP):
                code = table[chunk * GROUP + j]
                left.append(group[code & (CODE - 1)])
                right.append(store[code >> CODE_BITS])
            total[rows[chunk]] += lax.dot_general(
                jnp.concatenate(left, 1),
                jnp.concatenate(right, 1),
                (((1,), (1,)), ((), ())),
                preferred_element_type=jnp.float32,
            )
        return carry

    lax.fori_loop(0, trips, step, 0)


def own_kernel(table, rows, totals, own, store, total, group, sems):
    total[...] = jnp.zeros_like(total)
    multiply(table, rows, totals[0], (own,), store, group, sems, total)


def side_kernel(table, rows, totals, *refs):
    parts, (store, start, total, group, sems) = refs[:4], refs[4:]
    total[...] = start[...]
    multiply(table, rows, totals[1], parts, store, group, sems, total)


def far_kernel(scale, table, rows, totals, low, high, store, start, known, *refs):
    out, inner, group, sems, total = refs
    total[...] = start[...]
    multiply(table, rows, totals[2], (low, high), store, group, sems, total)
    product = jnp.concatenate([total[r] for r in range(total.shape[0])], 1)
    out[...] = product
    width = product.shape[0]
    both = jnp.concatenate([dot_nt(product, known[...]), dot_nt(product, product)], 1) * scale
    lanes = inner.shape[1]
    for n in range(0, both.shape[1], lanes):
        piece = both[:, n : n + lanes]
        row = n // lanes * width
        inner[row : row + width, : piece.shape[1]] = piece
        if piece.shape[1] < lanes:
            inner[row : row + width, piece.shape[1] :] = jnp.zeros(
                (width, lanes - piece.shape[1]), jnp.float32
            )


def apply_tiles(store, prepared, own, known, scale):
    block_rows, _, size, _ = store.shape
    store = store.reshape(-1, size, size)
    width = own.shape[2]
    vmem, smem = pl.BlockSpec(memory_space=pltpu.VMEM), pl.BlockSpec(memory_space=pltpu.SMEM)
    anywhere = pl.BlockSpec(memory_space=pl.ANY)
    total = jax.ShapeDtypeStruct((block_rows, width, size), jnp.float32)

    def flat(parts):
        return [p.reshape((-1,) + p.shape[2:]) for p in parts]

    def scratch(parts):
        held = sum(p.shape[0] for p in parts) + 1
        return [
            pltpu.VMEM((held,) + parts[0].shape[1:], parts[0].dtype),
            pltpu.SemaphoreType.DMA((len(parts),)),
        ]

    def shared(mib):
        return dict(
            compiler_params=pltpu.CompilerParams(vmem_limit_bytes=16 << 20),
            cost_estimate=pl.CostEstimate(
                flops=1 << 28, bytes_accessed=mib << 20, transcendentals=0
            ),
        )

    onward, rest = gather_beside(own)
    parts = flat((own,))
    start = pl.pallas_call(
        own_kernel,
        out_shape=total,
        in_specs=[smem] * 3 + [anywhere, vmem],
        out_specs=vmem,
        scratch_shapes=scratch(parts),
        name="own_tiles",
        **shared(8),
    )(*prepared[0], *parts, store)
    onward, start = lax.optimization_barrier((onward, start))
    beyond = gather_beyond(onward)
    parts = flat((rest[1], onward[1], onward[0], rest[0]))
    start = pl.pallas_call(
        side_kernel,
        out_shape=total,
        in_specs=[smem] * 3 + [anywhere] * 4 + [vmem] * 2,
        out_specs=vmem,
        scratch_shapes=scratch(parts),
        name="side_tiles",
        **shared(10),
    )(*prepared[1], *parts, store, start)
    parts = flat(beyond)
    pieces = -(-(known.shape[0] + width) // size)
    return pl.pallas_call(
        functools.partial(far_kernel, scale),
        out_shape=(
            jax.ShapeDtypeStruct((width, block_rows * size), jnp.float32),
            jax.ShapeDtypeStruct((pieces * width, size), jnp.float32),
        ),
        in_specs=[smem] * 3 + [anywhere] * 2 + [vmem] * 3,
        out_specs=(vmem, vmem),
        scratch_shapes=scratch(parts) + [pltpu.VMEM(total.shape, total.dtype)],
        name="far_tiles",
        **shared(8),
    )(*prepared[2], *parts, store, start, known)


def factor(gram):
    n = gram.shape[0]
    across = 2 * n
    row_ids = lax.broadcasted_iota(jnp.int32, (n, n), 0)
    col_ids = lax.broadcasted_iota(jnp.int32, (n, n), 1)
    eye = jnp.where(row_ids == col_ids, 1.0, 0.0).astype(jnp.float32)
    wide = jnp.concatenate([gram, eye], 1)
    parts = [wide[i : i + SUB] for i in range(0, n, SUB)]
    sub = lax.broadcasted_iota(jnp.int32, (SUB, across), 0)

    def lane(a, k):
        return jnp.broadcast_to(a[:, k : k + 1], (SUB, across))

    for k in range(0, n, PIVOTS):
        home, at = divmod(k, SUB)
        rows = [
            jnp.broadcast_to(parts[home][at + i : at + i + 1], (SUB, across))
            for i in range(PIVOTS)
        ]
        head = [[lane(rows[i], k + j) if i <= j else None for j in range(PIVOTS)] for i in range(PIVOTS)]
        inv = []
        for i in range(PIVOTS):
            inv.append(1.0 / head[i][i])
            for j in range(i + 1, PIVOTS):
                link = head[i][j] * inv[i]
                rows[j] = rows[j] - link * rows[i]
                for m in range(j, PIVOTS):
                    head[j][m] = head[j][m] - link * head[i][m]
        for i in range(home, len(parts)):
            links = []
            for j in range(PIVOTS):
                link = lane(parts[i], k + j)
                for m in range(j):
                    link = link - links[m] * head[m][j]
                links.append(link * inv[j])
            for j in range(PIVOTS):
                link = jnp.where(sub > at + j, links[j], 0.0) if i == home else links[j]
                parts[i] = parts[i] - link * rows[j]
    wide = jnp.concatenate(parts, 0)
    upper = wide[:, :n]
    diag = jnp.sum(jnp.where(row_ids == col_ids, upper, 0.0), 1, keepdims=True)
    scale = lax.rsqrt(diag)
    upper = jnp.where(row_ids <= col_ids, upper * scale, 0.0)
    lower = jnp.where(row_ids >= col_ids, wide[:, n:] * scale, 0.0)
    return upper, lower


def block_of(ref, i, b):
    return ref[i // 2 * b : (i // 2 + 1) * b, i % 2 * b : (i % 2 + 1) * b]


def known_inner(sums, prev, b):
    table, n = {}, 0
    for i in range(prev):
        for j in range(i, prev):
            table[i, j] = block_of(sums, n, b)
            n += 1
    rows = []
    for i in range(prev):
        row = [table[i, j] if i <= j else table[j, i].T for j in range(prev)]
        rows.append(jnp.concatenate(row, 1))
    return jnp.concatenate(rows, 0)


def first_kernel(sums, product, known, fresh, half, upper, cross):
    b = product.shape[0]
    prev = known.shape[0] // b
    count = prev * (prev + 1) // 2
    own = known_inner(sums, prev, b)
    proj = jnp.concatenate([block_of(sums, count + i, b) for i in range(prev)], 1)
    spread = dot_nn(proj, own)
    gram = block_of(sums, count + prev, b) + dot_nt(spread - 2.0 * proj, proj)
    residual = product[...] - dot_nn(proj, known[...])
    up, inverse = factor(gram)
    new = dot_nn(inverse, residual)
    fresh[...] = new
    upper[...] = up
    cross[...] = dot_nn(inverse, proj - spread)
    size = half.shape[2]
    for i in range(half.shape[0]):
        half[i] = new[:, i * size : (i + 1) * size].astype(half.dtype)


def last_kernel(sums, later, cross, product, known, fresh, first_upper, out, uppers):
    b = product.shape[0]
    prev = known.shape[0] // b
    own = known_inner(sums, prev, b)
    old = jnp.concatenate([block_of(later, i, b) for i in range(prev)], 1)
    new = block_of(later, prev, b)
    spread = dot_nn(old, own) + dot_nn(new, cross[...])
    spread_new = dot_nt(old, cross[...]) + new
    gram = (
        block_of(later, prev + 1, b)
        + dot_nt(spread - 2.0 * old, old)
        + dot_nt(spread_new - 2.0 * new, new)
    )
    residual = product[...] - dot_nn(old, known[...]) - dot_nn(new, fresh[...])
    up, inverse = factor(gram)
    out[0] = fresh[...]
    out[1] = dot_nn(inverse, residual)
    uppers[0] = first_upper[...]
    uppers[1] = up


def on_device(tiles, block_columns, live_counts, earlier):
    block_rows, slots, size, _ = tiles.shape
    prev, b, rows_here = earlier.shape
    scale = 1.0 / (rows_here * lax.axis_size("row") * lax.axis_size("col"))
    counts = live_counts.reshape(block_rows)
    here_y = lax.axis_index("col") // NZ
    owner = block_columns // block_rows
    turn = (owner // NZ - here_y) % NY
    picks = (turn * NZ + owner % NZ) * block_rows + block_columns % block_rows
    picks = picks.reshape(-1)
    vmem = pl.BlockSpec(memory_space=pltpu.VMEM)
    f32 = jnp.float32
    known = earlier.reshape(prev * b, rows_here)
    prepared = prepare(picks, counts, slots)

    def split(a):
        return jnp.transpose(a.reshape(b, block_rows, size), (1, 0, 2))

    own = to_all(split(earlier[-1].astype(jnp.bfloat16)), "col", NZ, Z_GROUPS)
    own, prepared = lax.optimization_barrier((own, prepared))
    inner = jnp.dot(known, known.T, precision=HI) * scale
    blocks = [
        inner[i * b : (i + 1) * b, j * b : (j + 1) * b]
        for i in range(prev)
        for j in range(i, prev)
    ]
    old = [jnp.concatenate(blocks[i : i + 2], 1) for i in range(0, len(blocks), 2)]
    product, mixed = apply_tiles(tiles, prepared, own, known, scale)
    sums = sum_everywhere(jnp.concatenate(old + [mixed], 0))
    fresh, half, upper, cross = pl.pallas_call(
        first_kernel,
        out_shape=(
            jax.ShapeDtypeStruct((b, rows_here), f32),
            jax.ShapeDtypeStruct((block_rows, b, size), jnp.bfloat16),
            jax.ShapeDtypeStruct((b, b), f32),
            jax.ShapeDtypeStruct((b, prev * b), f32),
        ),
        in_specs=[vmem] * 3,
        out_specs=(vmem,) * 4,
        compiler_params=pltpu.CompilerParams(vmem_limit_bytes=20 << 20),
        name="first_step",
    )(sums, product, known)

    own = to_all(half, "col", NZ, Z_GROUPS)
    basis = jnp.concatenate([known, fresh], 0)
    product, mixed = apply_tiles(tiles, prepared, own, basis, scale)
    mixed = jnp.concatenate([mixed, jnp.zeros((256 - mixed.shape[0], size), f32)], 0)
    later = sum_everywhere(mixed)
    return pl.pallas_call(
        last_kernel,
        out_shape=(
            jax.ShapeDtypeStruct((STEPS, b, rows_here), f32),
            jax.ShapeDtypeStruct((STEPS, b, b), f32),
        ),
        in_specs=[vmem] * 7,
        out_specs=(vmem, vmem),
        compiler_params=pltpu.CompilerParams(vmem_limit_bytes=20 << 20),
        name="last_step",
    )(sums, later, cross, product, known, fresh, upper)


def solution(mesh):
    return jax.shard_map(
        on_device,
        mesh=mesh,
        in_specs=(
            P(("row", "col"), None, None, None),
            P(("row", "col"), None),
            P("row", "col"),
            P(None, None, ("row", "col")),
        ),
        out_specs=(P(None, None, ("row", "col")), P()),
        check_vma=False,
    )
```

```python
import functools

import jax
import jax.numpy as jnp
from jax import lax
from jax.experimental import pallas as pl
from jax.experimental.pallas import tpu as pltpu
from jax.sharding import PartitionSpec as P

STEPS = 2
NX, NY, NZ, NC = 4, 4, 8, 2
SUB = 8
PIVOTS = 8
GROUP, GROUP_BITS = 4, 2
AT_ONCE, TRIP_BITS = 8, 5
VECTORS, VECTOR_BITS = 32, 5
DEAD = (VECTORS, 2 * VECTORS, VECTORS)
CODE, CODE_BITS = 128, 7
HI = lax.Precision.HIGHEST


def col_id(y, z):
    return (y % NY) * NZ + z % NZ


def row_id(x, core):
    return (x % NX) * NC + core % NC


Y_UP = [(col_id(y, z), col_id(y + 1, z)) for y in range(NY) for z in range(NZ)]
Y_DOWN = [(col_id(y, z), col_id(y - 1, z)) for y in range(NY) for z in range(NZ)]
Z_GROUPS = [[col_id(y, z) for z in range(NZ)] for y in range(NY)]
PLANES = [
    [
        row_id(x, c) * NY * NZ + col_id(y, z)
        for x in range(NX)
        for y in range(NY)
        for c in range(NC)
    ]
    for z in range(NZ)
]
ALL = ("row", "col")


def to_all(a, axis, count, groups=None):
    copies = jnp.broadcast_to(a[None], (count,) + a.shape)
    return lax.all_to_all(copies, axis, 0, 0, axis_index_groups=groups, tiled=True)


def spread_kernel(latest, out):
    size = out.shape[3]
    for i in range(out.shape[1]):
        block = latest[0, :, i * size : (i + 1) * size].astype(out.dtype)
        for n in range(out.shape[0]):
            out[n, i] = block


def spread_latest(earlier, size):
    prev, b, rows = earlier.shape
    out = (NZ, rows // size, b, size)
    return pl.pallas_call(
        spread_kernel,
        out_shape=jax.ShapeDtypeStruct(out, jnp.bfloat16),
        grid=(1,),
        in_specs=[pl.BlockSpec((1, b, rows), lambda i: (prev - 1, 0, 0))],
        out_specs=pl.BlockSpec(out, lambda i: (0, 0, 0, 0)),
        name="spread_latest",
    )(earlier)


def along_z(copies):
    return lax.all_to_all(copies, "col", 0, 0, axis_index_groups=Z_GROUPS, tiled=True)


def gather_beside(own):
    first, last = own[: NZ // 2], own[NZ // 2 :]
    onward = lax.ppermute(first, "col", Y_UP), lax.ppermute(last, "col", Y_DOWN)
    rest = lax.ppermute(last, "col", Y_UP), lax.ppermute(first, "col", Y_DOWN)
    return onward, rest


def gather_beyond(onward):
    return lax.ppermute(onward[0], "col", Y_UP), lax.ppermute(onward[1], "col", Y_DOWN)


def sum_everywhere(a):
    members = NX * NY * NC
    part = a.reshape(members, a.shape[0] // members, a.shape[1])
    piece = lax.all_to_all(part, ALL, 0, 0, axis_index_groups=PLANES, tiled=True)
    piece = jnp.sum(piece, 0)
    piece = jnp.sum(to_all(piece, "col", NZ, Z_GROUPS), 0)
    return to_all(piece, ALL, members, PLANES).reshape(a.shape)


def dot_nt(a, b):
    return lax.dot_general(
        a, b, (((1,), (1,)), ((), ())), precision=HI, preferred_element_type=jnp.float32
    )


def dot_nn(a, b):
    return lax.dot_general(
        a, b, (((1,), (0,)), ((), ())), precision=HI, preferred_element_type=jnp.float32
    )


def prepare_kernel(slots, picks, counts, *refs):
    block_rows = counts.shape[0]
    tables, rows, totals = refs[:3], refs[3:6], refs[6]

    def sort(r, ends):
        def one(s, ends):
            pick = picks[r * slots + s]
            turn = pick >> VECTOR_BITS
            tile = (r * slots + s) * CODE + (pick & (VECTORS - 1))
            tables[0][ends[0]] = tile
            tables[1][ends[1]] = tile + ((turn >> 1) << VECTOR_BITS)
            tables[2][ends[2]] = tile
            return (
                ends[0] + jnp.where(turn == 0, 1, 0),
                ends[1] + (turn & 1),
                ends[2] + jnp.where(turn == 2, 1, 0),
            )

        starts, stops = ends, []
        ends = lax.fori_loop(0, counts[r], one, ends)
        for table, row, start, end, dead in zip(tables, rows, starts, ends, DEAD):
            for j in range(GROUP):
                table[end + j] = r * slots * CODE + dead
            stop = (end + GROUP - 1) >> GROUP_BITS

            def mark(c, _, row=row):
                row[c] = r
                return 0

            lax.fori_loop(start >> GROUP_BITS, stop, mark, 0)
            stops.append(stop << GROUP_BITS)
        return tuple(stops)

    ends = lax.fori_loop(0, block_rows, sort, (jnp.int32(0),) * 3)
    for n, (table, row, end, dead) in enumerate(zip(tables, rows, ends, DEAD)):
        for j in range(GROUP * AT_ONCE):
            table[end + j] = dead
        for j in range(AT_ONCE):
            row[(end >> GROUP_BITS) + j] = 0
        totals[n] = (end + GROUP * AT_ONCE - 1) >> TRIP_BITS


def prepare(picks, counts, slots):
    block_rows = counts.shape[0]
    smem = pl.BlockSpec(memory_space=pltpu.SMEM)
    entries = block_rows * (slots + GROUP) + 2 * GROUP * AT_ONCE
    table = jax.ShapeDtypeStruct((entries,), jnp.int32)
    rows = jax.ShapeDtypeStruct((entries // GROUP,), jnp.int32)
    out = pl.pallas_call(
        functools.partial(prepare_kernel, slots),
        out_shape=(table,) * 3 + (rows,) * 3 + (jax.ShapeDtypeStruct((3,), jnp.int32),),
        in_specs=[smem, smem],
        out_specs=(smem,) * 7,
        compiler_params=pltpu.CompilerParams(vmem_limit_bytes=16 << 20),
        cost_estimate=pl.CostEstimate(flops=0, bytes_accessed=8 << 20, transcendentals=0),
        name="prepare",
    )(picks, counts)
    return [(out[n], out[3 + n], out[6]) for n in range(3)]


def multiply(table, rows, trips, parts, store, group, sems, total):
    copies, start = [], 0
    for n, part in enumerate(parts):
        at = pl.ds(start, part.shape[0])
        copies.append(pltpu.make_async_copy(part, group.at[at], sems.at[n]))
        start += part.shape[0]
    for c in copies:
        c.start()
    group[start] = jnp.zeros(group.shape[1:], group.dtype)
    for c in copies:
        c.wait()

    def step(t, carry):
        for c in range(AT_ONCE):
            chunk = t * AT_ONCE + c
            left, right = [], []
            for j in range(GROUP):
                code = table[chunk * GROUP + j]
                left.append(group[code & (CODE - 1)])
                right.append(store[code >> CODE_BITS])
            total[rows[chunk]] += lax.dot_general(
                jnp.concatenate(left, 1),
                jnp.concatenate(right, 1),
                (((1,), (1,)), ((), ())),
                preferred_element_type=jnp.float32,
            )
        return carry

    lax.fori_loop(0, trips, step, 0)


def own_kernel(table, rows, totals, own, store, total, group, sems):
    total[...] = jnp.zeros_like(total)
    multiply(table, rows, totals[0], (own,), store, group, sems, total)


def side_kernel(table, rows, totals, *refs):
    parts, (store, start, total, group, sems) = refs[:4], refs[4:]
    total[...] = start[...]
    multiply(table, rows, totals[1], parts, store, group, sems, total)


def far_kernel(scale, table, rows, totals, low, high, store, start, known, *refs):
    out, inner, group, sems, total = refs
    total[...] = start[...]
    multiply(table, rows, totals[2], (low, high), store, group, sems, total)
    product = jnp.concatenate([total[r] for r in range(total.shape[0])], 1)
    out[...] = product
    width = product.shape[0]
    both = jnp.concatenate([dot_nt(product, known[...]), dot_nt(product, product)], 1) * scale
    lanes = inner.shape[1]
    for n in range(0, both.shape[1], lanes):
        piece = both[:, n : n + lanes]
        row = n // lanes * width
        inner[row : row + width, : piece.shape[1]] = piece
        if piece.shape[1] < lanes:
            inner[row : row + width, piece.shape[1] :] = jnp.zeros(
                (width, lanes - piece.shape[1]), jnp.float32
            )


def apply_tiles(store, prepared, own, known, scale):
    block_rows, _, size, _ = store.shape
    store = store.reshape(-1, size, size)
    width = own.shape[2]
    vmem, smem = pl.BlockSpec(memory_space=pltpu.VMEM), pl.BlockSpec(memory_space=pltpu.SMEM)
    anywhere = pl.BlockSpec(memory_space=pl.ANY)
    total = jax.ShapeDtypeStruct((block_rows, width, size), jnp.float32)

    def flat(parts):
        return [p.reshape((-1,) + p.shape[2:]) for p in parts]

    def scratch(parts):
        held = sum(p.shape[0] for p in parts) + 1
        return [
            pltpu.VMEM((held,) + parts[0].shape[1:], parts[0].dtype),
            pltpu.SemaphoreType.DMA((len(parts),)),
        ]

    def shared(mib):
        return dict(
            compiler_params=pltpu.CompilerParams(vmem_limit_bytes=16 << 20),
            cost_estimate=pl.CostEstimate(
                flops=1 << 28, bytes_accessed=mib << 20, transcendentals=0
            ),
        )

    onward, rest = gather_beside(own)
    parts = flat((own,))
    start = pl.pallas_call(
        own_kernel,
        out_shape=total,
        in_specs=[smem] * 3 + [anywhere, vmem],
        out_specs=vmem,
        scratch_shapes=scratch(parts),
        name="own_tiles",
        **shared(8),
    )(*prepared[0], *parts, store)
    onward, start = lax.optimization_barrier((onward, start))
    beyond = gather_beyond(onward)
    parts = flat((rest[1], onward[1], onward[0], rest[0]))
    start = pl.pallas_call(
        side_kernel,
        out_shape=total,
        in_specs=[smem] * 3 + [anywhere] * 4 + [vmem] * 2,
        out_specs=vmem,
        scratch_shapes=scratch(parts),
        name="side_tiles",
        **shared(10),
    )(*prepared[1], *parts, store, start)
    parts = flat(beyond)
    pieces = -(-(known.shape[0] + width) // size)
    return pl.pallas_call(
        functools.partial(far_kernel, scale),
        out_shape=(
            jax.ShapeDtypeStruct((width, block_rows * size), jnp.float32),
            jax.ShapeDtypeStruct((pieces * width, size), jnp.float32),
        ),
        in_specs=[smem] * 3 + [anywhere] * 2 + [vmem] * 3,
        out_specs=(vmem, vmem),
        scratch_shapes=scratch(parts) + [pltpu.VMEM(total.shape, total.dtype)],
        name="far_tiles",
        **shared(8),
    )(*prepared[2], *parts, store, start, known)


def factor(gram):
    n = gram.shape[0]
    across = 2 * n
    row_ids = lax.broadcasted_iota(jnp.int32, (n, n), 0)
    col_ids = lax.broadcasted_iota(jnp.int32, (n, n), 1)
    eye = jnp.where(row_ids == col_ids, 1.0, 0.0).astype(jnp.float32)
    wide = jnp.concatenate([gram, eye], 1)
    parts = [wide[i : i + SUB] for i in range(0, n, SUB)]
    sub = lax.broadcasted_iota(jnp.int32, (SUB, across), 0)

    def lane(a, k):
        return jnp.broadcast_to(a[:, k : k + 1], (SUB, across))

    for k in range(0, n, PIVOTS):
        home, at = divmod(k, SUB)
        rows = [
            jnp.broadcast_to(parts[home][at + i : at + i + 1], (SUB, across))
            for i in range(PIVOTS)
        ]
        head = [[lane(rows[i], k + j) if i <= j else None for j in range(PIVOTS)] for i in range(PIVOTS)]
        inv = []
        for i in range(PIVOTS):
            inv.append(1.0 / head[i][i])
            for j in range(i + 1, PIVOTS):
                link = head[i][j] * inv[i]
                rows[j] = rows[j] - link * rows[i]
                for m in range(j, PIVOTS):
                    head[j][m] = head[j][m] - link * head[i][m]
        for i in range(home, len(parts)):
            links = []
            for j in range(PIVOTS):
                link = lane(parts[i], k + j)
                for m in range(j):
                    link = link - links[m] * head[m][j]
                links.append(link * inv[j])
            for j in range(PIVOTS):
                link = jnp.where(sub > at + j, links[j], 0.0) if i == home else links[j]
                parts[i] = parts[i] - link * rows[j]
    wide = jnp.concatenate(parts, 0)
    upper = wide[:, :n]
    diag = jnp.sum(jnp.where(row_ids == col_ids, upper, 0.0), 1, keepdims=True)
    scale = lax.rsqrt(diag)
    upper = jnp.where(row_ids <= col_ids, upper * scale, 0.0)
    lower = jnp.where(row_ids >= col_ids, wide[:, n:] * scale, 0.0)
    return upper, lower


def block_of(ref, i, b):
    return ref[i // 2 * b : (i // 2 + 1) * b, i % 2 * b : (i % 2 + 1) * b]


def known_inner(sums, prev, b):
    table, n = {}, 0
    for i in range(prev):
        for j in range(i, prev):
            table[i, j] = block_of(sums, n, b)
            n += 1
    rows = []
    for i in range(prev):
        row = [table[i, j] if i <= j else table[j, i].T for j in range(prev)]
        rows.append(jnp.concatenate(row, 1))
    return jnp.concatenate(rows, 0)


def first_kernel(sums, product, known, fresh, half, upper, cross):
    b = product.shape[0]
    prev = known.shape[0] // b
    count = prev * (prev + 1) // 2
    own = known_inner(sums, prev, b)
    proj = jnp.concatenate([block_of(sums, count + i, b) for i in range(prev)], 1)
    spread = dot_nn(proj, own)
    gram = block_of(sums, count + prev, b) + dot_nt(spread - 2.0 * proj, proj)
    residual = product[...] - dot_nn(proj, known[...])
    up, inverse = factor(gram)
    new = dot_nn(inverse, residual)
    fresh[...] = new
    upper[...] = up
    cross[...] = dot_nn(inverse, proj - spread)
    size = half.shape[3]
    for i in range(half.shape[1]):
        block = new[:, i * size : (i + 1) * size].astype(half.dtype)
        for n in range(half.shape[0]):
            half[n, i] = block


def last_kernel(sums, later, cross, product, known, fresh, first_upper, out, uppers):
    b = product.shape[0]
    prev = known.shape[0] // b
    own = known_inner(sums, prev, b)
    old = jnp.concatenate([block_of(later, i, b) for i in range(prev)], 1)
    new = block_of(later, prev, b)
    spread = dot_nn(old, own) + dot_nn(new, cross[...])
    spread_new = dot_nt(old, cross[...]) + new
    gram = (
        block_of(later, prev + 1, b)
        + dot_nt(spread - 2.0 * old, old)
        + dot_nt(spread_new - 2.0 * new, new)
    )
    residual = product[...] - dot_nn(old, known[...]) - dot_nn(new, fresh[...])
    up, inverse = factor(gram)
    out[0] = fresh[...]
    out[1] = dot_nn(inverse, residual)
    uppers[0] = first_upper[...]
    uppers[1] = up


def on_device(tiles, block_columns, live_counts, earlier):
    block_rows, slots, size, _ = tiles.shape
    prev, b, rows_here = earlier.shape
    scale = 1.0 / (rows_here * lax.axis_size("row") * lax.axis_size("col"))
    counts = live_counts.reshape(block_rows)
    here_y = lax.axis_index("col") // NZ
    owner = block_columns // block_rows
    turn = (owner // NZ - here_y) % NY
    picks = (turn * NZ + owner % NZ) * block_rows + block_columns % block_rows
    picks = picks.reshape(-1)
    vmem = pl.BlockSpec(memory_space=pltpu.VMEM)
    f32 = jnp.float32
    known = earlier.reshape(prev * b, rows_here)
    prepared = prepare(picks, counts, slots)

    own = along_z(spread_latest(earlier, size))
    own, prepared = lax.optimization_barrier((own, prepared))
    inner = jnp.dot(known, known.T, precision=HI) * scale
    blocks = [
        inner[i * b : (i + 1) * b, j * b : (j + 1) * b]
        for i in range(prev)
        for j in range(i, prev)
    ]
    old = [jnp.concatenate(blocks[i : i + 2], 1) for i in range(0, len(blocks), 2)]
    product, mixed = apply_tiles(tiles, prepared, own, known, scale)
    sums = sum_everywhere(jnp.concatenate(old + [mixed], 0))
    fresh, half, upper, cross = pl.pallas_call(
        first_kernel,
        out_shape=(
            jax.ShapeDtypeStruct((b, rows_here), f32),
            jax.ShapeDtypeStruct((NZ, block_rows, b, size), jnp.bfloat16),
            jax.ShapeDtypeStruct((b, b), f32),
            jax.ShapeDtypeStruct((b, prev * b), f32),
        ),
        in_specs=[vmem] * 3,
        out_specs=(vmem,) * 4,
        compiler_params=pltpu.CompilerParams(vmem_limit_bytes=20 << 20),
        name="first_step",
    )(sums, product, known)

    own = along_z(half)
    basis = jnp.concatenate([known, fresh], 0)
    product, mixed = apply_tiles(tiles, prepared, own, basis, scale)
    mixed = jnp.concatenate([mixed, jnp.zeros((256 - mixed.shape[0], size), f32)], 0)
    later = sum_everywhere(mixed)
    return pl.pallas_call(
        last_kernel,
        out_shape=(
            jax.ShapeDtypeStruct((STEPS, b, rows_here), f32),
            jax.ShapeDtypeStruct((STEPS, b, b), f32),
        ),
        in_specs=[vmem] * 7,
        out_specs=(vmem, vmem),
        compiler_params=pltpu.CompilerParams(vmem_limit_bytes=20 << 20),
        name="last_step",
    )(sums, later, cross, product, known, fresh, upper)


def solution(mesh):
    return jax.shard_map(
        on_device,
        mesh=mesh,
        in_specs=(
            P(("row", "col"), None, None, None),
            P(("row", "col"), None),
            P("row", "col"),
            P(None, None, ("row", "col")),
        ),
        out_specs=(P(None, None, ("row", "col")), P()),
        check_vma=False,
    )
```

```python
import functools

import jax
import jax.numpy as jnp
from jax import lax
from jax.experimental import pallas as pl
from jax.experimental.pallas import tpu as pltpu
from jax.sharding import PartitionSpec as P

STEPS = 2
NX, NY, NZ, NC = 4, 4, 8, 2
SUB = 8
PIVOTS = 8
GROUP, GROUP_BITS = 4, 2
AT_ONCE, TRIP_BITS = 8, 5
VECTORS, VECTOR_BITS = 32, 5
DEAD = (VECTORS, 2 * VECTORS, VECTORS)
CODE, CODE_BITS = 128, 7
HI = lax.Precision.HIGHEST


def col_id(y, z):
    return (y % NY) * NZ + z % NZ


def row_id(x, core):
    return (x % NX) * NC + core % NC


Y_UP = [(col_id(y, z), col_id(y + 1, z)) for y in range(NY) for z in range(NZ)]
Y_DOWN = [(col_id(y, z), col_id(y - 1, z)) for y in range(NY) for z in range(NZ)]
Z_GROUPS = [[col_id(y, z) for z in range(NZ)] for y in range(NY)]
PLANES = [
    [
        row_id(x, c) * NY * NZ + col_id(y, z)
        for x in range(NX)
        for y in range(NY)
        for c in range(NC)
    ]
    for z in range(NZ)
]
ALL = ("row", "col")


def to_all(a, axis, count, groups=None):
    copies = jnp.broadcast_to(a[None], (count,) + a.shape)
    return lax.all_to_all(copies, axis, 0, 0, axis_index_groups=groups, tiled=True)


def spread_kernel(latest, out):
    size = out.shape[3]
    for i in range(out.shape[1]):
        block = latest[0, :, i * size : (i + 1) * size].astype(out.dtype)
        for n in range(out.shape[0]):
            out[n, i] = block


def spread_latest(earlier, size):
    prev, b, rows = earlier.shape
    out = (NZ, rows // size, b, size)
    return pl.pallas_call(
        spread_kernel,
        out_shape=jax.ShapeDtypeStruct(out, jnp.bfloat16),
        grid=(1,),
        in_specs=[pl.BlockSpec((1, b, rows), lambda i: (prev - 1, 0, 0))],
        out_specs=pl.BlockSpec(out, lambda i: (0, 0, 0, 0)),
        name="spread_latest",
    )(earlier)


def along_z(copies):
    return lax.all_to_all(copies, "col", 0, 0, axis_index_groups=Z_GROUPS, tiled=True)


def gather_beside(own):
    first, last = own[: NZ // 2], own[NZ // 2 :]
    onward = lax.ppermute(first, "col", Y_UP), lax.ppermute(last, "col", Y_DOWN)
    rest = lax.ppermute(last, "col", Y_UP), lax.ppermute(first, "col", Y_DOWN)
    return onward, rest


def gather_beyond(onward):
    return lax.ppermute(onward[0], "col", Y_UP), lax.ppermute(onward[1], "col", Y_DOWN)


def sum_everywhere(a):
    members = NX * NY * NC
    part = a.reshape(members, a.shape[0] // members, a.shape[1])
    piece = lax.all_to_all(part, ALL, 0, 0, axis_index_groups=PLANES, tiled=True)
    piece = jnp.sum(piece, 0)
    piece = jnp.sum(to_all(piece, "col", NZ, Z_GROUPS), 0)
    return to_all(piece, ALL, members, PLANES).reshape(a.shape)


def dot_nt(a, b):
    return lax.dot_general(
        a, b, (((1,), (1,)), ((), ())), precision=HI, preferred_element_type=jnp.float32
    )


def dot_nn(a, b):
    return lax.dot_general(
        a, b, (((1,), (0,)), ((), ())), precision=HI, preferred_element_type=jnp.float32
    )


def prepare_kernel(slots, picks, counts, *refs):
    block_rows = counts.shape[0]
    tables, rows, totals = refs[:3], refs[3:6], refs[6]

    def sort(r, ends):
        def one(s, ends):
            pick = picks[r * slots + s]
            turn = pick >> VECTOR_BITS
            tile = (r * slots + s) * CODE + (pick & (VECTORS - 1))
            tables[0][ends[0]] = tile
            tables[1][ends[1]] = tile + ((turn >> 1) << VECTOR_BITS)
            tables[2][ends[2]] = tile
            return (
                ends[0] + jnp.where(turn == 0, 1, 0),
                ends[1] + (turn & 1),
                ends[2] + jnp.where(turn == 2, 1, 0),
            )

        starts, stops = ends, []
        ends = lax.fori_loop(0, counts[r], one, ends)
        for table, row, start, end, dead in zip(tables, rows, starts, ends, DEAD):
            for j in range(GROUP):
                table[end + j] = r * slots * CODE + dead
            stop = (end + GROUP - 1) >> GROUP_BITS

            def mark(c, _, row=row):
                row[c] = r
                return 0

            lax.fori_loop(start >> GROUP_BITS, stop, mark, 0)
            stops.append(stop << GROUP_BITS)
        return tuple(stops)

    ends = lax.fori_loop(0, block_rows, sort, (jnp.int32(0),) * 3)
    for n, (table, row, end, dead) in enumerate(zip(tables, rows, ends, DEAD)):
        for j in range(GROUP * AT_ONCE):
            table[end + j] = dead
        for j in range(AT_ONCE):
            row[(end >> GROUP_BITS) + j] = 0
        totals[n] = (end + GROUP * AT_ONCE - 1) >> TRIP_BITS


def prepare(picks, counts, slots):
    block_rows = counts.shape[0]
    smem = pl.BlockSpec(memory_space=pltpu.SMEM)
    entries = block_rows * (slots + GROUP) + 2 * GROUP * AT_ONCE
    table = jax.ShapeDtypeStruct((entries,), jnp.int32)
    rows = jax.ShapeDtypeStruct((entries // GROUP,), jnp.int32)
    out = pl.pallas_call(
        functools.partial(prepare_kernel, slots),
        out_shape=(table,) * 3 + (rows,) * 3 + (jax.ShapeDtypeStruct((3,), jnp.int32),),
        in_specs=[smem, smem],
        out_specs=(smem,) * 7,
        compiler_params=pltpu.CompilerParams(vmem_limit_bytes=16 << 20),
        cost_estimate=pl.CostEstimate(flops=0, bytes_accessed=8 << 20, transcendentals=0),
        name="prepare",
    )(picks, counts)
    return [(out[n], out[3 + n], out[6]) for n in range(3)]


def multiply(table, rows, trips, parts, store, group, sems, total):
    copies, start = [], 0
    for n, part in enumerate(parts):
        at = pl.ds(start, part.shape[0])
        copies.append(pltpu.make_async_copy(part, group.at[at], sems.at[n]))
        start += part.shape[0]
    for c in copies:
        c.start()
    group[start] = jnp.zeros(group.shape[1:], group.dtype)
    for c in copies:
        c.wait()

    def step(t, carry):
        for c in range(AT_ONCE):
            chunk = t * AT_ONCE + c
            left, right = [], []
            for j in range(GROUP):
                code = table[chunk * GROUP + j]
                left.append(group[code & (CODE - 1)])
                right.append(store[code >> CODE_BITS])
            total[rows[chunk]] += lax.dot_general(
                jnp.concatenate(left, 1),
                jnp.concatenate(right, 1),
                (((1,), (1,)), ((), ())),
                preferred_element_type=jnp.float32,
            )
        return carry

    lax.fori_loop(0, trips, step, 0)


def own_kernel(table, rows, totals, own, store, total, group, sems):
    total[...] = jnp.zeros_like(total)
    multiply(table, rows, totals[0], (own,), store, group, sems, total)


def side_kernel(table, rows, totals, *refs):
    parts, (store, start, total, group, sems) = refs[:4], refs[4:]
    total[...] = start[...]
    multiply(table, rows, totals[1], parts, store, group, sems, total)


def far_kernel(scale, table, rows, totals, low, high, store, start, known, *refs):
    out, inner, group, sems, total = refs
    total[...] = start[...]
    multiply(table, rows, totals[2], (low, high), store, group, sems, total)
    product = jnp.concatenate([total[r] for r in range(total.shape[0])], 1)
    out[...] = product
    width = product.shape[0]
    both = jnp.concatenate([dot_nt(product, known[...]), dot_nt(product, product)], 1) * scale
    lanes = inner.shape[1]
    for n in range(0, both.shape[1], lanes):
        piece = both[:, n : n + lanes]
        row = n // lanes * width
        inner[row : row + width, : piece.shape[1]] = piece
        if piece.shape[1] < lanes:
            inner[row : row + width, piece.shape[1] :] = jnp.zeros(
                (width, lanes - piece.shape[1]), jnp.float32
            )


def apply_tiles(store, prepared, own, known, scale):
    block_rows, _, size, _ = store.shape
    store = store.reshape(-1, size, size)
    width = own.shape[2]
    vmem, smem = pl.BlockSpec(memory_space=pltpu.VMEM), pl.BlockSpec(memory_space=pltpu.SMEM)
    anywhere = pl.BlockSpec(memory_space=pl.ANY)
    total = jax.ShapeDtypeStruct((block_rows, width, size), jnp.float32)

    def flat(parts):
        return [p.reshape((-1,) + p.shape[2:]) for p in parts]

    def scratch(parts):
        held = sum(p.shape[0] for p in parts) + 1
        return [
            pltpu.VMEM((held,) + parts[0].shape[1:], parts[0].dtype),
            pltpu.SemaphoreType.DMA((len(parts),)),
        ]

    def shared(mib):
        return dict(
            compiler_params=pltpu.CompilerParams(vmem_limit_bytes=16 << 20),
            cost_estimate=pl.CostEstimate(
                flops=1 << 28, bytes_accessed=mib << 20, transcendentals=0
            ),
        )

    onward, rest = gather_beside(own)
    parts = flat((own,))
    start = pl.pallas_call(
        own_kernel,
        out_shape=total,
        in_specs=[smem] * 3 + [anywhere, vmem],
        out_specs=vmem,
        scratch_shapes=scratch(parts),
        name="own_tiles",
        **shared(8),
    )(*prepared[0], *parts, store)
    onward, start = lax.optimization_barrier((onward, start))
    beyond = gather_beyond(onward)
    parts = flat((rest[1], onward[1], onward[0], rest[0]))
    start = pl.pallas_call(
        side_kernel,
        out_shape=total,
        in_specs=[smem] * 3 + [anywhere] * 4 + [vmem] * 2,
        out_specs=vmem,
        scratch_shapes=scratch(parts),
        name="side_tiles",
        **shared(10),
    )(*prepared[1], *parts, store, start)
    parts = flat(beyond)
    pieces = -(-(known.shape[0] + width) // size)
    return pl.pallas_call(
        functools.partial(far_kernel, scale),
        out_shape=(
            jax.ShapeDtypeStruct((width, block_rows * size), jnp.float32),
            jax.ShapeDtypeStruct((pieces * width, size), jnp.float32),
        ),
        in_specs=[smem] * 3 + [anywhere] * 2 + [vmem] * 3,
        out_specs=(vmem, vmem),
        scratch_shapes=scratch(parts) + [pltpu.VMEM(total.shape, total.dtype)],
        name="far_tiles",
        **shared(8),
    )(*prepared[2], *parts, store, start, known)


def factor(gram):
    n = gram.shape[0]
    across = 2 * n
    row_ids = lax.broadcasted_iota(jnp.int32, (n, n), 0)
    col_ids = lax.broadcasted_iota(jnp.int32, (n, n), 1)
    eye = jnp.where(row_ids == col_ids, 1.0, 0.0).astype(jnp.float32)
    wide = jnp.concatenate([gram, eye], 1)
    parts = [wide[i : i + SUB] for i in range(0, n, SUB)]
    sub = lax.broadcasted_iota(jnp.int32, (SUB, across), 0)

    def lane(a, k):
        return jnp.broadcast_to(a[:, k : k + 1], (SUB, across))

    for k in range(0, n, PIVOTS):
        home, at = divmod(k, SUB)
        rows = [
            jnp.broadcast_to(parts[home][at + i : at + i + 1], (SUB, across))
            for i in range(PIVOTS)
        ]
        head = [[lane(rows[i], k + j) if i <= j else None for j in range(PIVOTS)] for i in range(PIVOTS)]
        inv = []
        for i in range(PIVOTS):
            inv.append(1.0 / head[i][i])
            for j in range(i + 1, PIVOTS):
                link = head[i][j] * inv[i]
                rows[j] = rows[j] - link * rows[i]
                for m in range(j, PIVOTS):
                    head[j][m] = head[j][m] - link * head[i][m]
        for i in range(home, len(parts)):
            links = []
            for j in range(PIVOTS):
                link = lane(parts[i], k + j)
                for m in range(j):
                    link = link - links[m] * head[m][j]
                links.append(link * inv[j])
            for j in range(PIVOTS):
                link = jnp.where(sub > at + j, links[j], 0.0) if i == home else links[j]
                parts[i] = parts[i] - link * rows[j]
    wide = jnp.concatenate(parts, 0)
    upper = wide[:, :n]
    diag = jnp.sum(jnp.where(row_ids == col_ids, upper, 0.0), 1, keepdims=True)
    scale = lax.rsqrt(diag)
    upper = jnp.where(row_ids <= col_ids, upper * scale, 0.0)
    lower = jnp.where(row_ids >= col_ids, wide[:, n:] * scale, 0.0)
    return upper, lower


def block_of(ref, i, b):
    return ref[i // 2 * b : (i // 2 + 1) * b, i % 2 * b : (i % 2 + 1) * b]


def known_inner(sums, prev, b):
    table, n = {}, 0
    for i in range(prev):
        for j in range(i, prev):
            table[i, j] = block_of(sums, n, b)
            n += 1
    rows = []
    for i in range(prev):
        row = [table[i, j] if i <= j else table[j, i].T for j in range(prev)]
        rows.append(jnp.concatenate(row, 1))
    return jnp.concatenate(rows, 0)


def first_kernel(sums, product, known, fresh, half, upper, cross):
    b = product.shape[0]
    prev = known.shape[0] // b
    count = prev * (prev + 1) // 2
    own = known_inner(sums, prev, b)
    proj = jnp.concatenate([block_of(sums, count + i, b) for i in range(prev)], 1)
    spread = dot_nn(proj, own)
    gram = block_of(sums, count + prev, b) + dot_nt(spread - 2.0 * proj, proj)
    residual = product[...] - dot_nn(proj, known[...])
    up, inverse = factor(gram)
    new = dot_nn(inverse, residual)
    fresh[...] = new
    upper[...] = up
    cross[...] = dot_nn(inverse, proj - spread)
    size = half.shape[3]
    for i in range(half.shape[1]):
        block = new[:, i * size : (i + 1) * size].astype(half.dtype)
        for n in range(half.shape[0]):
            half[n, i] = block


def last_kernel(sums, later, cross, product, known, fresh, first_upper, out, uppers):
    b = product.shape[0]
    prev = known.shape[0] // b
    own = known_inner(sums, prev, b)
    old = jnp.concatenate([block_of(later, i, b) for i in range(prev)], 1)
    new = block_of(later, prev, b)
    proj = jnp.concatenate([old, new], 1)
    spread = dot_nn(proj, jnp.concatenate([own, cross[...]], 0))
    spread_new = dot_nt(old, cross[...]) + new
    spread = jnp.concatenate([spread, spread_new], 1)
    gram = block_of(later, prev + 1, b) + dot_nt(spread - 2.0 * proj, proj)
    residual = product[...] - dot_nn(old, known[...]) - dot_nn(new, fresh[...])
    up, inverse = factor(gram)
    out[0] = fresh[...]
    out[1] = dot_nn(inverse, residual)
    uppers[0] = first_upper[...]
    uppers[1] = up


def on_device(tiles, block_columns, live_counts, earlier):
    block_rows, slots, size, _ = tiles.shape
    prev, b, rows_here = earlier.shape
    scale = 1.0 / (rows_here * lax.axis_size("row") * lax.axis_size("col"))
    counts = live_counts.reshape(block_rows)
    here_y = lax.axis_index("col") // NZ
    owner = block_columns // block_rows
    turn = (owner // NZ - here_y) % NY
    picks = (turn * NZ + owner % NZ) * block_rows + block_columns % block_rows
    picks = picks.reshape(-1)
    vmem = pl.BlockSpec(memory_space=pltpu.VMEM)
    f32 = jnp.float32
    known = earlier.reshape(prev * b, rows_here)
    prepared = prepare(picks, counts, slots)

    own = along_z(spread_latest(earlier, size))
    own, prepared = lax.optimization_barrier((own, prepared))
    inner = jnp.dot(known, known.T, precision=HI) * scale
    blocks = [
        inner[i * b : (i + 1) * b, j * b : (j + 1) * b]
        for i in range(prev)
        for j in range(i, prev)
    ]
    old = [jnp.concatenate(blocks[i : i + 2], 1) for i in range(0, len(blocks), 2)]
    product, mixed = apply_tiles(tiles, prepared, own, known, scale)
    sums = sum_everywhere(jnp.concatenate(old + [mixed], 0))
    fresh, half, upper, cross = pl.pallas_call(
        first_kernel,
        out_shape=(
            jax.ShapeDtypeStruct((b, rows_here), f32),
            jax.ShapeDtypeStruct((NZ, block_rows, b, size), jnp.bfloat16),
            jax.ShapeDtypeStruct((b, b), f32),
            jax.ShapeDtypeStruct((b, prev * b), f32),
        ),
        in_specs=[vmem] * 3,
        out_specs=(vmem,) * 4,
        compiler_params=pltpu.CompilerParams(vmem_limit_bytes=20 << 20),
        name="first_step",
    )(sums, product, known)

    own = along_z(half)
    basis = jnp.concatenate([known, fresh], 0)
    product, mixed = apply_tiles(tiles, prepared, own, basis, scale)
    mixed = jnp.concatenate([mixed, jnp.zeros((256 - mixed.shape[0], size), f32)], 0)
    later = sum_everywhere(mixed)
    return pl.pallas_call(
        last_kernel,
        out_shape=(
            jax.ShapeDtypeStruct((STEPS, b, rows_here), f32),
            jax.ShapeDtypeStruct((STEPS, b, b), f32),
        ),
        in_specs=[vmem] * 7,
        out_specs=(vmem, vmem),
        compiler_params=pltpu.CompilerParams(vmem_limit_bytes=20 << 20),
        name="last_step",
    )(sums, later, cross, product, known, fresh, upper)


def solution(mesh):
    return jax.shard_map(
        on_device,
        mesh=mesh,
        in_specs=(
            P(("row", "col"), None, None, None),
            P(("row", "col"), None),
            P("row", "col"),
            P(None, None, ("row", "col")),
        ),
        out_specs=(P(None, None, ("row", "col")), P()),
        check_vma=False,
    )
```
